32 devices in a mesh: dp: 8 (over y, x, core), tensor: 4 (over z).
Axes of the slice: x: 2, y: 2, z: 4, core: 2. Of those that a mesh axis runs over, the one named last changes fastest.
Arguments:
- enc_hidden: bfloat16 [16384, 4096], P(('dp', 'tensor')), parts along dimension 0, may hold values from -6 to 6
- enc_gain: float32 [4096], replicated, may hold values from 0.1 to 1.9
- dec_hidden: bfloat16 [4096, 4096], P(('dp', 'tensor')), parts along dimension 0, may hold values from -6 to 6
- dec_gain: float32 [4096], replicated, may hold values from 0.8 to 12, as said below
- w_query: bfloat16 [4096, 4096], P(None, 'tensor'), may hold values from -0.046875 to 0.046875
- w_key: bfloat16 [4096, 4096], P(None, 'tensor'), may hold values from -0.09375 to 0.09375
- w_value: bfloat16 [4096, 4096], P(None, 'tensor'), may hold values from -0.09375 to 0.09375
- w_out: bfloat16 [4096, 4096], P('tensor'), may hold values from -0.75 to 0.75
- enc_length: int32 [8], P('dp'), parts along dimension 0, may hold values from 1024 to 2048
- dec_length: int32 [8], P('dp'), parts along dimension 0, may hold values from 256 to 512
Outputs:
- memory: bfloat16 [16384, 4096], P(('dp', 'tensor')), parts along dimension 0
- cross_out: bfloat16 [4096, 4096], P(('dp', 'tensor')), parts along dimension 0
The draws below stay inside these ranges and needn't reach their ends.
There are 8 independent parts, one for each index of `dp`. The reference program is written for one: setup_inputs(seed, part) draws one part's arguments, and reference() takes and returns one part's arrays. A program takes and returns all parts, laid end to end along the dimension named above; an argument that names none is the same for every part. Nothing has to cross between parts.
Inputs may be any that keep to these rules, and one draw needn't show every extreme that they name: `dec_gain`: positive.
All inputs are finite; a program needn't handle non-finite values.
Results may differ from the reference program's by a relative error of at most 0.02.
The reference program's roundings to bfloat16 on the way count: a program that leaves them out, or rounds other values in their place, can miss the bound.
Values may be sent and summed in bfloat16 or wider, within the bound.
No kernel may reach another device: no remote copies, remote signals or barrier semaphores. Data moves between devices by JAX's collectives and lax.ppermute only.
A program may use at most 192 MiB of HBM per device.

```python
import jax
import jax.numpy as jnp
from jax import lax

D = 4096
HEADS = 64
HEAD_DIM = 64
ENC_LEN = 2048
DEC_LEN = 512
HD = 4096
N_TENSOR = 4


def draw_dec_gain(key, part):
    return jax.random.uniform(key, (D,), jnp.float32, 0.8, 1.2)


def levels(key, extent, split, low, high):
    def one(position, parts):
        heights = jax.random.uniform(jax.random.fold_in(jax.random.fold_in(key, 6), position), (parts,), jnp.float32, low / len(split), high / len(split))
        return jnp.repeat(jnp.exp(heights), extent[position] // parts).reshape((-1,) + (1,) * (len(extent) - position - 1))

    factor_of = one(*split[0])
    for cut in split[1:]:
        factor_of = factor_of * one(*cut)
    return factor_of


def noise(rng, shape, scale, limit, split=(), kind=jnp.bfloat16):
    level = levels(rng, shape, split, -0.22, 0.18) if split else 1.0
    array = jax.random.normal(rng, shape, jnp.float32) * scale * level
    return jnp.minimum(jnp.maximum(array, -limit), limit).astype(kind)


def setup_inputs(seed: int = 0, part: int = 0) -> dict:
    streams_of = jax.random.split(jax.random.key(seed), 11)
    part_splits = jax.random.split(jax.random.fold_in(streams_of[10], part), 11)
    return {
        "enc_hidden": noise(part_splits[0], (ENC_LEN, D), 1.0, 6.0, ((0, 4),)),
        "enc_gain": jnp.clip(1.0 + 0.18 * jax.random.normal(streams_of[1], (D,), jnp.float32), 0.1, 1.9),
        "dec_hidden": noise(part_splits[2], (DEC_LEN, D), 1.0, 6.0, ((0, 4),)),
        "dec_gain": draw_dec_gain(jax.random.fold_in(streams_of[10], 71), part),
        "w_query": noise(streams_of[4], (D, HD), (4 * D) ** -0.5, 0.046875, ((1, 4),)),
        "w_key": noise(streams_of[5], (D, HD), D ** -0.5, 0.09375, ((1, 4),)),
        "w_value": noise(streams_of[6], (D, HD), D ** -0.5, 0.09375, ((1, 4),)),
        "w_out": noise(streams_of[7], (HD, D), HEAD_DIM ** -0.5, 0.75, ((0, 4),)),
        "enc_length": jax.random.randint(part_splits[8], (1,), ENC_LEN // 2, ENC_LEN + 1).astype(jnp.int32),
        "dec_length": jax.random.randint(part_splits[9], (1,), DEC_LEN // 2, DEC_LEN + 1).astype(jnp.int32),
    }


def rms_norm(values, gain):
    wide = values.astype(jnp.float32)
    mean_sq = lax.optimization_barrier(jnp.mean(wide * wide, axis=-1, keepdims=True))
    return (wide * jax.lax.rsqrt(mean_sq + 1e-06) * gain.astype(jnp.float32)).astype(jnp.bfloat16)

def reference(enc_hidden, enc_gain, dec_hidden, dec_gain, w_query, w_key, w_value, w_out, enc_length, dec_length):
    memory = rms_norm(enc_hidden, enc_gain)
    normed = rms_norm(dec_hidden, dec_gain)
    queries = jnp.dot(normed, w_query, preferred_element_type=jnp.float32).astype(jnp.bfloat16)
    key_rows = jnp.dot(memory, w_key, preferred_element_type=jnp.float32).astype(jnp.bfloat16)
    value_rows = jnp.dot(memory, w_value, preferred_element_type=jnp.float32).astype(jnp.bfloat16)
    q_heads = queries.reshape(DEC_LEN, HEADS, HEAD_DIM).astype(jnp.float32)
    k_heads = key_rows.reshape(ENC_LEN, HEADS, HEAD_DIM).astype(jnp.float32)
    v_heads = value_rows.reshape(ENC_LEN, HEADS, HEAD_DIM).astype(jnp.float32)
    scores = jnp.einsum('qhd,khd->hqk', q_heads, k_heads)
    valid_keys = jnp.arange(ENC_LEN, dtype=jnp.int32) < enc_length[0]
    scores = jnp.where(valid_keys[None, None, :], scores, -jnp.inf)
    weights = jax.nn.softmax(scores, axis=-1).astype(jnp.bfloat16)
    context = jnp.einsum('hqk,khd->qhd', weights.astype(jnp.float32), v_heads)
    context = context.astype(jnp.bfloat16).reshape(DEC_LEN, HD)
    group_width = HD // N_TENSOR
    context_groups = context.reshape(DEC_LEN, N_TENSOR, group_width).transpose(1, 0, 2)
    out_groups = w_out.reshape(N_TENSOR, group_width, D)

    def add_group(total, pair):
        ctx_part, out_part = pair
        partial_value = jnp.dot(ctx_part, out_part, preferred_element_type=jnp.float32)
        partial_value = partial_value.astype(jnp.bfloat16).astype(jnp.float32)
        return (total + partial_value, None)
    projected, _ = lax.scan(add_group, jnp.zeros((DEC_LEN, D), jnp.float32), (context_groups, out_groups))
    live_rows = jnp.arange(DEC_LEN, dtype=jnp.int32) < dec_length[0]
    cross_out = jnp.where(live_rows[:, None], projected, 0.0).astype(jnp.bfloat16)
    return (memory, cross_out)
```

```python
import functools

import jax
import jax.numpy as jnp
from jax import lax
from jax.experimental import pallas as pl
from jax.experimental.pallas import tpu as pltpu
from jax.sharding import PartitionSpec as P

HEAD_DIM = 64
LANES = 128
MASKED = -1e30


def rms_norm(values, gain):
    wide = values.astype(jnp.float32)
    mean_sq = jnp.mean(wide * wide, axis=-1, keepdims=True)
    return (wide * lax.rsqrt(mean_sq + 1e-06) * gain).astype(jnp.bfloat16)


def project(rows, weight):
    return jnp.dot(rows, weight, preferred_element_type=jnp.float32).astype(jnp.bfloat16)


def after(value, *others):
    return lax.optimization_barrier((value,) + others)[0]


def attend_kernel(pieces, q_ref, mask_ref, *refs):
    k_refs, v_refs = refs[:pieces], refs[pieces : 2 * pieces]
    o_ref, stat_ref = refs[2 * pieces :]
    pair = pl.program_id(0)
    queries = q_ref[...]
    lane = lax.broadcasted_iota(jnp.int32, queries.shape, 1)
    low = lane < HEAD_DIM
    keys = k_refs[0].shape[0]
    outs, stats = [], []
    for head in range(2):
        mine = low if head == 0 else jnp.logical_not(low)
        q_head = jnp.where(mine, queries, jnp.zeros_like(queries))
        scores = []
        for i in range(pieces):
            s = lax.dot_general(
                q_head, k_refs[i][...], (((1,), (1,)), ((), ())), preferred_element_type=jnp.float32
            )
            scores.append(s + mask_ref[:, i * keys : (i + 1) * keys])
        top = scores[0].max(axis=-1, keepdims=True)
        for s in scores[1:]:
            top = jnp.maximum(top, s.max(axis=-1, keepdims=True))
        total, out = None, None
        for i in range(pieces):
            p = jnp.exp(scores[i] - top)
            t = p.sum(axis=-1, keepdims=True)
            o = jnp.dot(p.astype(jnp.bfloat16), v_refs[i][...], preferred_element_type=jnp.float32)
            total = t if total is None else total + t
            out = o if out is None else out + o
        outs.append(out / total)
        stats.append(top + jnp.log(total))
    o_ref[...] = jnp.where(low, outs[0], outs[1]).astype(jnp.bfloat16)

    @pl.when(pair == 0)
    def _():
        stat_ref[...] = jnp.zeros_like(stat_ref)

    held = stat_ref[...]
    held = jnp.where(lane == 2 * pair, stats[0], held)
    stat_ref[...] = jnp.where(lane == 2 * pair + 1, stats[1], held)


def attend(queries, block, rows, keys, values, mask):
    width = keys[0].shape[1]
    pieces, depth = len(keys), keys[0].shape[0]
    kv = pl.BlockSpec((depth, LANES), lambda i: (0, i))
    return pl.pallas_call(
        functools.partial(attend_kernel, pieces),
        grid=(width // LANES,),
        in_specs=[
            pl.BlockSpec((rows, LANES), lambda i: (block, i)),
            pl.BlockSpec((1, pieces * depth), lambda i: (0, 0)),
        ]
        + [kv] * (2 * pieces),
        out_specs=[
            pl.BlockSpec((rows, LANES), lambda i: (0, i)),
            pl.BlockSpec((rows, LANES), lambda i: (0, 0)),
        ],
        out_shape=[
            jax.ShapeDtypeStruct((rows, width), jnp.bfloat16),
            jax.ShapeDtypeStruct((rows, LANES), jnp.float32),
        ],
        name="attend",
    )(queries, mask, *keys, *values)


def merge_kernel(a_ref, b_ref, sa_ref, sb_ref, o_ref):
    rows, width = a_ref.shape
    sa, sb = sa_ref[...], sb_ref[...]
    top = jnp.maximum(sa, sb)
    ea, eb = jnp.exp(sa - top), jnp.exp(sb - top)
    share = ea / (ea + eb)
    low = lax.broadcasted_iota(jnp.int32, (rows, LANES), 1) < HEAD_DIM
    for pair in range(width // LANES):
        at = slice(pair * LANES, (pair + 1) * LANES)
        wa = jnp.where(low, share[:, 2 * pair : 2 * pair + 1], share[:, 2 * pair + 1 : 2 * pair + 2])
        a, b = a_ref[:, at].astype(jnp.float32), b_ref[:, at].astype(jnp.float32)
        o_ref[:, at] = (b + wa * (a - b)).astype(jnp.bfloat16)


def merge(mine, theirs):
    (a, sa), (b, sb) = mine, theirs
    return pl.pallas_call(
        merge_kernel, out_shape=jax.ShapeDtypeStruct(a.shape, jnp.bfloat16), name="merge"
    )(a, b, sa, sb)


def make_shards(n, nd):
    half = n // 2
    partner = [(i, (i + half) % n) for i in range(n)]

    def within(step):
        return [(i, i // half * half + (i % half + step) % half) for i in range(n)]

    def swap(x):
        return lax.ppermute(x, "tensor", partner)

    def to_place(x, step):
        return lax.ppermute(x, "tensor", within(step))

    def flip(x, bits):
        return lax.ppermute(x, "dp", [(i, i ^ bits) for i in range(nd)])

    def fetch_piece(w, index):
        rows = w.shape[0] // nd
        return swap(lax.dynamic_slice_in_dim(w, index * rows, rows, 0))

    def spread(piece, index):
        if nd & (nd - 1):
            return lax.all_gather(piece, "dp", axis=0, tiled=True)
        rows = piece.shape[0]
        held = {0: piece}
        for j in range(2, nd, 2):
            held[j] = flip(piece, j)
        for j in range(0, nd, 2):
            held[j ^ 1] = flip(held[j], 1)
        whole = jnp.zeros((rows * nd, piece.shape[1]), piece.dtype)
        for j in range(nd):
            whole = lax.dynamic_update_slice_in_dim(whole, held[j], (index ^ j) * rows, 0)
        return whole

    def shards(
        enc_hidden,
        enc_gain,
        dec_hidden,
        dec_gain,
        w_query,
        w_key,
        w_value,
        w_out,
        enc_length,
        dec_length,
    ):
        place = lax.axis_index("tensor")
        index = lax.axis_index("dp")
        a, b = place // half, place % half
        enc_rows, dec_rows = enc_hidden.shape[0], dec_hidden.shape[0]

        normed = rms_norm(dec_hidden, dec_gain)
        normed_far = swap(normed)
        memory = rms_norm(enc_hidden, enc_gain)

        key_piece = fetch_piece(w_key, index)
        value_piece = fetch_piece(w_value, index)
        out_piece = fetch_piece(w_out, index)

        near = [normed] + [to_place(normed, s) for s in range(1, half)]
        far = [normed_far] + [to_place(normed_far, s) for s in range(1, half)]
        memories = [memory] + [to_place(memory, s) for s in range(1, half)]
        q_rows = half * dec_rows
        queries = project(jnp.concatenate(near + far, axis=0), w_query)
        queries_far = swap(queries)

        first = (a * half + (b - jnp.arange(half)) % half) * enc_rows
        key_ids = first[:, None] + jnp.arange(enc_rows)[None, :]
        mask = jnp.where(key_ids < enc_length[0], 0.0, MASKED).astype(jnp.float32).reshape(1, -1)

        keys = [project(m, w_key) for m in memories]
        values = [project(m, w_value) for m in memories]
        sent_own = attend(queries, 1, q_rows, keys, values, mask)
        theirs_far = [swap(x) for x in sent_own]
        kept_own = attend(queries, 0, q_rows, keys, values, mask)

        w_key_far = spread(key_piece, index)
        w_value_far = spread(value_piece, index)
        keys_far = [project(m, w_key_far) for m in memories]
        values_far = [project(m, w_value_far) for m in memories]
        sent_far = attend(queries_far, 0, q_rows, keys_far, values_far, mask)
        theirs_own = [swap(x) for x in sent_far]
        kept_far = attend(queries_far, 1, q_rows, keys_far, values_far, mask)

        w_out_far = spread(out_piece, index)
        context_far = merge(kept_far, theirs_far)
        context_own = merge(kept_own, theirs_own)

        def partial(step):
            at = slice(step * dec_rows, (step + 1) * dec_rows)
            return jnp.dot(context_own[at], w_out, preferred_element_type=jnp.float32) + jnp.dot(
                context_far[at], w_out_far, preferred_element_type=jnp.float32
            )

        total = None
        for step in range(1, half):
            got = to_place(partial(step).astype(jnp.bfloat16), half - step).astype(jnp.float32)
            total = got if total is None else total + got
        mine = partial(0).astype(jnp.bfloat16).astype(jnp.float32)
        total = mine if total is None else total + mine
        row_ids = place * dec_rows + jnp.arange(dec_rows, dtype=jnp.int32)
        live_rows = row_ids < dec_length[0]
        cross_out = jnp.where(live_rows[:, None], total, 0.0).astype(jnp.bfloat16)
        return (memory, cross_out)

    return shards


def solution(mesh):
    placed = (
        P(("dp", "tensor"), None),
        P(),
        P(("dp", "tensor"), None),
        P(),
        P(None, "tensor"),
        P(None, "tensor"),
        P(None, "tensor"),
        P("tensor", None),
        P("dp"),
        P("dp"),
    )
    return jax.shard_map(
        make_shards(mesh.shape["tensor"], mesh.shape["dp"]),
        mesh=mesh,
        in_specs=placed,
        out_specs=(P(("dp", "tensor"), None), P(("dp", "tensor"), None)),
        check_vma=False,
    )
```
